32 devices in a mesh: stream: 2 (over y), batch: 16 (over z, x, core).
Axes of the slice: x: 2, y: 2, z: 4, core: 2. Of those that a mesh axis runs over, the one named last changes fastest.
Arguments:
- text_states: bfloat16 [128, 128, 768], P(('stream', 'batch')), may hold values from -6 to 6
- image_states: bfloat16 [128, 36, 1024], P(('stream', 'batch')), may hold values from -6 to 6
- caption_lengths: int32 [128], P(('stream', 'batch')), may hold values from 8 to 128, as said below
- region_counts: int32 [128], P(('stream', 'batch')), may hold values from 10 to 36, as said below
- text_cotangent: bfloat16 [128, 128, 768], P(('stream', 'batch')), may hold values from -6 to 6
- image_cotangent: bfloat16 [128, 36, 1024], P(('stream', 'batch')), may hold values from -6 to 6
- text_query: bfloat16 [768, 1024], P(('stream', 'batch')), may hold values from -0.21875 to 0.21875
- text_keyvalue: bfloat16 [768, 2048], P(('stream', 'batch')), may hold values from -0.21875 to 0.21875
- text_output: bfloat16 [1024, 768], P(('stream', 'batch')), may hold values from -0.75 to 0.75
- text_up: bfloat16 [768, 3072], P(('stream', 'batch')), may hold values from -0.21875 to 0.21875
- text_down: bfloat16 [3072, 768], P(('stream', 'batch')), may hold values from -0.109375 to 0.109375
- text_norm1_gain: bfloat16 [768], P(('stream', 'batch')), may hold values from 0.25 to 1.75
- text_norm1_bias: bfloat16 [768], P(('stream', 'batch')), may hold values from -1.1953125 to 1.1953125
- text_norm2_gain: bfloat16 [768], P(('stream', 'batch')), may hold values from 0.25 to 1.75
- text_norm2_bias: bfloat16 [768], P(('stream', 'batch')), may hold values from -1.1953125 to 1.1953125
- text_self_qkv: bfloat16 [768, 2304], P(('stream', 'batch')), may hold values from -0.21875 to 0.21875
- text_self_output: bfloat16 [768, 768], P(('stream', 'batch')), may hold values from -0.875 to 0.875
- text_norm0_gain: bfloat16 [768], P(('stream', 'batch')), may hold values from 0.25 to 1.75
- text_norm0_bias: bfloat16 [768], P(('stream', 'batch')), may hold values from -1.1953125 to 1.1953125
- image_query: bfloat16 [1024, 1024], P(('stream', 'batch')), may hold values from -0.1875 to 0.1875
- image_keyvalue: bfloat16 [1024, 2048], P(('stream', 'batch')), may hold values from -0.1875 to 0.1875
- image_output: bfloat16 [1024, 1024], P(('stream', 'batch')), may hold values from -0.75 to 0.75
- image_up: bfloat16 [1024, 1024], P(('stream', 'batch')), may hold values from -0.1875 to 0.1875
- image_down: bfloat16 [1024, 1024], P(('stream', 'batch')), may hold values from -0.1875 to 0.1875
- image_norm1_gain: bfloat16 [1024], P(('stream', 'batch')), may hold values from 0.25 to 1.75
- image_norm1_bias: bfloat16 [1024], P(('stream', 'batch')), may hold values from -1.1953125 to 1.1953125
- image_norm2_gain: bfloat16 [1024], P(('stream', 'batch')), may hold values from 0.25 to 1.75
- image_norm2_bias: bfloat16 [1024], P(('stream', 'batch')), may hold values from -1.1953125 to 1.1953125
- image_self_qkv: bfloat16 [1024, 3072], P(('stream', 'batch')), may hold values from -0.1875 to 0.1875
- image_self_output: bfloat16 [1024, 1024], P(('stream', 'batch')), may hold values from -0.5 to 0.5
- image_norm0_gain: bfloat16 [1024], P(('stream', 'batch')), may hold values from 0.25 to 1.75
- image_norm0_bias: bfloat16 [1024], P(('stream', 'batch')), may hold values from -1.1953125 to 1.1953125
Outputs:
- text_result: bfloat16 [128, 128, 768], P(('stream', 'batch'))
- image_result: bfloat16 [128, 36, 1024], P(('stream', 'batch'))
- text_states_grad: float32 [128, 128, 768], P(('stream', 'batch'))
- image_states_grad: float32 [128, 36, 1024], P(('stream', 'batch'))
- text_query_grad: float32 [768, 1024], P(('stream', 'batch'))
- text_keyvalue_grad: float32 [768, 2048], P(('stream', 'batch'))
- text_output_grad: float32 [1024, 768], P(('stream', 'batch'))
- text_up_grad: float32 [768, 3072], P(('stream', 'batch'))
- text_down_grad: float32 [3072, 768], P(('stream', 'batch'))
- text_norm1_gain_grad: float32 [768], P(('stream', 'batch'))
- text_norm1_bias_grad: float32 [768], P(('stream', 'batch'))
- text_norm2_gain_grad: float32 [768], P(('stream', 'batch'))
- text_norm2_bias_grad: float32 [768], P(('stream', 'batch'))
- text_self_qkv_grad: float32 [768, 2304], P(('stream', 'batch'))
- text_self_output_grad: float32 [768, 768], P(('stream', 'batch'))
- text_norm0_gain_grad: float32 [768], P(('stream', 'batch'))
- text_norm0_bias_grad: float32 [768], P(('stream', 'batch'))
- image_query_grad: float32 [1024, 1024], P(('stream', 'batch'))
- image_keyvalue_grad: float32 [1024, 2048], P(('stream', 'batch'))
- image_output_grad: float32 [1024, 1024], P(('stream', 'batch'))
- image_up_grad: float32 [1024, 1024], P(('stream', 'batch'))
- image_down_grad: float32 [1024, 1024], P(('stream', 'batch'))
- image_norm1_gain_grad: float32 [1024], P(('stream', 'batch'))
- image_norm1_bias_grad: float32 [1024], P(('stream', 'batch'))
- image_norm2_gain_grad: float32 [1024], P(('stream', 'batch'))
- image_norm2_bias_grad: float32 [1024], P(('stream', 'batch'))
- image_self_qkv_grad: float32 [1024, 3072], P(('stream', 'batch'))
- image_self_output_grad: float32 [1024, 1024], P(('stream', 'batch'))
- image_norm0_gain_grad: float32 [1024], P(('stream', 'batch'))
- image_norm0_bias_grad: float32 [1024], P(('stream', 'batch'))
The draws below stay inside these ranges and needn't reach their ends.
Inputs may be any that keep to these rules, and one draw needn't show every extreme that they name: `caption_lengths`: each pair's caption length comes from one of three sets, short, medium or long; some pair fills all 128 slots. `region_counts`: some pair has all 36 regions.
All inputs are finite; a program needn't handle non-finite values.
Results may differ from the reference program's by a relative error of at most 0.02.
Values may be sent and summed in bfloat16 or wider, within the bound.
No kernel may reach another device: no remote copies, remote signals or barrier semaphores. Data moves between devices by JAX's collectives and lax.ppermute only.
A program may use at most 320 MiB of HBM per device.

```python
import math
import jax
import jax.numpy as jnp
from jax import lax

TEXT_WIDTH = 768
TEXT_HIDDEN = 3072
IMAGE_WIDTH = 1024
IMAGE_HIDDEN = 1024
TEXT_HEADS = 12
IMAGE_HEADS = 8
HEADS = 8
INNER = 1024
SLOTS = 128
REGIONS = 36
PAIRS = 128


def draw_caption_lengths(key, part):
    sets = jax.random.randint(jax.random.fold_in(key, 11), (PAIRS,), 0, 3)
    lower = jnp.where(sets == 0, SLOTS // 16, jnp.where(sets == 1, SLOTS // 4, SLOTS // 2))
    upper = jnp.where(sets == 0, SLOTS // 4, jnp.where(sets == 1, SLOTS // 2, SLOTS + 1))
    raw = jax.random.randint(jax.random.fold_in(key, 12), (PAIRS,), 0, 1 << 20)
    drawn = lower + raw % (upper - lower)
    place = jax.random.randint(jax.random.fold_in(key, 13), (), 0, PAIRS)
    return jnp.where(jnp.arange(PAIRS) == place, SLOTS, drawn).astype(jnp.int32)


def draw_region_counts(key, part):
    lower = REGIONS * 5 // 18
    drawn = jax.random.randint(jax.random.fold_in(key, 21), (PAIRS,), lower, REGIONS + 1)
    place = jax.random.randint(jax.random.fold_in(key, 22), (), 0, PAIRS)
    return jnp.where(jnp.arange(PAIRS) == place, REGIONS, drawn).astype(jnp.int32)


def level_of(own_key, extent, cuts, low, top_value):
    level, own = 1.0, jax.random.fold_in(own_key, 6)
    for axis_at, parts in cuts:
        draws = jnp.exp(jax.random.uniform(jax.random.fold_in(own, axis_at), (parts,), jnp.float32, low / len(cuts), top_value / len(cuts)))
        level = level * jnp.repeat(draws, extent[axis_at] // parts).reshape([-1 if axis == axis_at else 1 for axis in range(len(extent))])
    return level


def gaussian(own_key, shape, deviation, most, shards=(), dtype=jnp.bfloat16):
    entries = deviation * jax.random.normal(own_key, shape, jnp.float32)
    if shards:
        entries = entries * level_of(own_key, shape, shards, -0.22, 0.18)
    return jnp.clip(entries, -most, most).astype(dtype)


def setup_inputs(seed: int = 0) -> dict:
    arg_keys = jax.random.split(jax.random.key(seed), 33)
    return {
        "text_states": gaussian(arg_keys[0], (PAIRS, SLOTS, TEXT_WIDTH), 1.0, 6.0, ((0, 32),)),
        "image_states": gaussian(arg_keys[1], (PAIRS, REGIONS, IMAGE_WIDTH), 1.0, 6.0, ((0, 32),)),
        "caption_lengths": draw_caption_lengths(jax.random.fold_in(arg_keys[32], 71), 0),
        "region_counts": draw_region_counts(jax.random.fold_in(arg_keys[32], 71), 0),
        "text_cotangent": gaussian(arg_keys[4], (PAIRS, SLOTS, TEXT_WIDTH), 1.0, 6.0, ((0, 32),)),
        "image_cotangent": gaussian(arg_keys[5], (PAIRS, REGIONS, IMAGE_WIDTH), 1.0, 6.0, ((0, 32),)),
        "text_query": gaussian(arg_keys[6], (TEXT_WIDTH, INNER), TEXT_WIDTH ** -0.5, 0.21875, ((0, 32),)),
        "text_keyvalue": gaussian(arg_keys[7], (TEXT_WIDTH, 2 * INNER), TEXT_WIDTH ** -0.5, 0.21875, ((0, 32),)),
        "text_output": gaussian(arg_keys[8], (INNER, TEXT_WIDTH), (INNER // 16) ** -0.5, 0.75, ((0, 32),)),
        "text_up": gaussian(arg_keys[9], (TEXT_WIDTH, TEXT_HIDDEN), TEXT_WIDTH ** -0.5, 0.21875, ((0, 32),)),
        "text_down": gaussian(arg_keys[10], (TEXT_HIDDEN, TEXT_WIDTH), TEXT_HIDDEN ** -0.5, 0.109375, ((0, 32),)),
        "text_norm1_gain": jnp.clip(1.0 + 0.15 * jax.random.normal(arg_keys[11], (TEXT_WIDTH,), jnp.float32), 0.25, 1.75).astype(jnp.bfloat16),
        "text_norm1_bias": gaussian(arg_keys[12], (TEXT_WIDTH,), 0.3, 1.1953125, ((0, 32),)),
        "text_norm2_gain": jnp.clip(1.0 + 0.15 * jax.random.normal(arg_keys[13], (TEXT_WIDTH,), jnp.float32), 0.25, 1.75).astype(jnp.bfloat16),
        "text_norm2_bias": gaussian(arg_keys[14], (TEXT_WIDTH,), 0.3, 1.1953125, ((0, 32),)),
        "text_self_qkv": gaussian(arg_keys[15], (TEXT_WIDTH, 3 * TEXT_WIDTH), TEXT_WIDTH ** -0.5, 0.21875, ((0, 32),)),
        "text_self_output": gaussian(arg_keys[16], (TEXT_WIDTH, TEXT_WIDTH), (TEXT_WIDTH // 16) ** -0.5, 0.875, ((0, 32),)),
        "text_norm0_gain": jnp.clip(1.0 + 0.15 * jax.random.normal(arg_keys[17], (TEXT_WIDTH,), jnp.float32), 0.25, 1.75).astype(jnp.bfloat16),
        "text_norm0_bias": gaussian(arg_keys[18], (TEXT_WIDTH,), 0.3, 1.1953125, ((0, 32),)),
        "image_query": gaussian(arg_keys[19], (IMAGE_WIDTH, INNER), IMAGE_WIDTH ** -0.5, 0.1875, ((0, 32),)),
        "image_keyvalue": gaussian(arg_keys[20], (IMAGE_WIDTH, 2 * INNER), IMAGE_WIDTH ** -0.5, 0.1875, ((0, 32),)),
        "image_output": gaussian(arg_keys[21], (INNER, IMAGE_WIDTH), (INNER // 16) ** -0.5, 0.75, ((0, 32),)),
        "image_up": gaussian(arg_keys[22], (IMAGE_WIDTH, IMAGE_HIDDEN), IMAGE_WIDTH ** -0.5, 0.1875, ((0, 32),)),
        "image_down": gaussian(arg_keys[23], (IMAGE_HIDDEN, IMAGE_WIDTH), IMAGE_HIDDEN ** -0.5, 0.1875, ((0, 32),)),
        "image_norm1_gain": jnp.clip(1.0 + 0.15 * jax.random.normal(arg_keys[24], (IMAGE_WIDTH,), jnp.float32), 0.25, 1.75).astype(jnp.bfloat16),
        "image_norm1_bias": gaussian(arg_keys[25], (IMAGE_WIDTH,), 0.3, 1.1953125, ((0, 32),)),
        "image_norm2_gain": jnp.clip(1.0 + 0.15 * jax.random.normal(arg_keys[26], (IMAGE_WIDTH,), jnp.float32), 0.25, 1.75).astype(jnp.bfloat16),
        "image_norm2_bias": gaussian(arg_keys[27], (IMAGE_WIDTH,), 0.3, 1.1953125, ((0, 32),)),
        "image_self_qkv": gaussian(arg_keys[28], (IMAGE_WIDTH, 3 * IMAGE_WIDTH), IMAGE_WIDTH ** -0.5, 0.1875, ((0, 32),)),
        "image_self_output": gaussian(arg_keys[29], (IMAGE_WIDTH, IMAGE_WIDTH), (IMAGE_WIDTH // 8) ** -0.5, 0.5, ((0, 32),)),
        "image_norm0_gain": jnp.clip(1.0 + 0.15 * jax.random.normal(arg_keys[30], (IMAGE_WIDTH,), jnp.float32), 0.25, 1.75).astype(jnp.bfloat16),
        "image_norm0_bias": gaussian(arg_keys[31], (IMAGE_WIDTH,), 0.3, 1.1953125, ((0, 32),)),
    }


HIGH = lax.Precision.HIGHEST
EPS = 1e-05
NEG = -1e+30

@jax.custom_vjp
def low(v):
    return lax.optimization_barrier(v.astype(jnp.bfloat16)).astype(jnp.float32)

@jax.custom_vjp
def low_back(v):
    return v

def low_keep(v):
    return (low(v), None)

def low_pass(kept, grad):
    return (grad,)

def back_keep(v):
    return (v, None)

def back_low(kept, grad):
    return (low(grad),)
low.defvjp(low_keep, low_pass)
low_back.defvjp(back_keep, back_low)

def product(left, right):
    return jnp.einsum('...i,ij->...j', left, right, precision=HIGH)

def layer_norm(values, gain, bias):
    mean = lax.optimization_barrier(jnp.mean(values, axis=-1, keepdims=True))
    centred = values - mean
    spread = lax.optimization_barrier(jnp.mean(centred * centred, axis=-1, keepdims=True))
    return centred * lax.rsqrt(spread + EPS) * gain + bias

def attend(query, keys, values, live, heads):
    pairs, rows, inner = query.shape
    count = keys.shape[1]
    size = inner // heads
    heads_q = query.reshape(pairs, rows, heads, size)
    heads_k = keys.reshape(pairs, count, heads, size)
    heads_v = values.reshape(pairs, count, heads, size)
    scores = jnp.einsum('pqhd,pkhd->phqk', heads_q, heads_k, precision=HIGH) * size ** (-0.5)
    scores = low_back(scores)
    scores = jnp.where(live[:, None, None, :], scores, NEG)
    probs = jax.nn.softmax(scores, axis=-1)
    mixed = jnp.einsum('phqk,pkhd->pqhd', low(probs), heads_v, precision=HIGH)
    return low_back(low(mixed.reshape(pairs, rows, inner)))

def self_block(states, weights, live, heads):
    width = states.shape[-1]
    qkv = low_back(low(product(states, weights[9])))
    mixed = attend(qkv[..., :width], qkv[..., width:2 * width], qkv[..., 2 * width:], live, heads)
    branch = low_back(product(mixed, weights[10]))
    return layer_norm(states + branch, weights[11], weights[12])

def stream(base, low_base, weights, key_values, live):
    inner = weights[0].shape[1]
    query = low_back(low(product(low_base, weights[0])))
    mixed = attend(query, key_values[..., :inner], key_values[..., inner:], live, HEADS)
    branch = low_back(product(mixed, weights[2]))
    hidden = layer_norm(base + branch, weights[5], weights[6])
    gate = low_back(product(low(hidden), weights[3]))
    active = low(jax.nn.gelu(gate, approximate=False))
    return layer_norm(hidden + low_back(product(active, weights[4])), weights[7], weights[8])

def forward(text, image, text_live, region_live, text_weights, image_weights):
    text_base = self_block(text, text_weights, text_live, TEXT_HEADS)
    image_base = self_block(image, image_weights, region_live, IMAGE_HEADS)
    text_low = low(text_base)
    image_low = low(image_base)
    text_kv = low_back(low(product(text_low, text_weights[1])))
    image_kv = low_back(low(product(image_low, image_weights[1])))
    return (stream(text_base, text_low, text_weights, image_kv, region_live), stream(image_base, image_low, image_weights, text_kv, text_live))

def reference(text_states, image_states, caption_lengths, region_counts, text_cotangent, image_cotangent, text_query, text_keyvalue, text_output, text_up, text_down, text_norm1_gain, text_norm1_bias, text_norm2_gain, text_norm2_bias, text_self_qkv, text_self_output, text_norm0_gain, text_norm0_bias, image_query, image_keyvalue, image_output, image_up, image_down, image_norm1_gain, image_norm1_bias, image_norm2_gain, image_norm2_bias, image_self_qkv, image_self_output, image_norm0_gain, image_norm0_bias):
    half = PAIRS // 2
    weights = tuple((piece.astype(jnp.float32) for piece in (text_query, text_keyvalue, text_output, text_up, text_down, text_norm1_gain, text_norm1_bias, text_norm2_gain, text_norm2_bias, text_self_qkv, text_self_output, text_norm0_gain, text_norm0_bias, image_query, image_keyvalue, image_output, image_up, image_down, image_norm1_gain, image_norm1_bias, image_norm2_gain, image_norm2_bias, image_self_qkv, image_self_output, image_norm0_gain, image_norm0_bias)))
    x_text = text_states.astype(jnp.float32)
    x_image = jnp.roll(image_states.astype(jnp.float32), half, axis=0)
    d_text = text_cotangent.astype(jnp.float32)
    d_image = jnp.roll(image_cotangent.astype(jnp.float32), half, axis=0)
    pair_regions = jnp.roll(region_counts, half, axis=0)
    text_live = lax.broadcasted_iota(jnp.int32, (PAIRS, SLOTS), 1) < caption_lengths[:, None]
    region_live = lax.broadcasted_iota(jnp.int32, (PAIRS, REGIONS), 1) < pair_regions[:, None]
    block = math.gcd(PAIRS, 32)
    blocks = PAIRS // block

    def whole(text, image, params):

        def one(items):
            return forward(items[0], items[1], items[2], items[3], params[:13], params[13:])
        shaped = (text.reshape(blocks, block, SLOTS, TEXT_WIDTH), image.reshape(blocks, block, REGIONS, IMAGE_WIDTH), text_live.reshape(blocks, block, SLOTS), region_live.reshape(blocks, block, REGIONS))
        out_text, out_image = lax.map(jax.checkpoint(one), shaped)
        return (out_text.reshape(PAIRS, SLOTS, TEXT_WIDTH), out_image.reshape(PAIRS, REGIONS, IMAGE_WIDTH))
    (y_text, y_image), pull = jax.vjp(whole, x_text, x_image, weights)
    g_text, g_image, grads = pull((d_text, d_image))
    return (y_text.astype(jnp.bfloat16), jnp.roll(y_image, half, axis=0).astype(jnp.bfloat16), g_text, jnp.roll(g_image, half, axis=0), grads[0], grads[1], grads[2], grads[3], grads[4], grads[5], grads[6], grads[7], grads[8], grads[9], grads[10], grads[11], grads[12], grads[13], grads[14], grads[15], grads[16], grads[17], grads[18], grads[19], grads[20], grads[21], grads[22], grads[23], grads[24], grads[25])
```

```python
import jax
import jax.numpy as jnp
from jax import lax
from jax.sharding import Mesh
from jax.sharding import PartitionSpec as P

TEXT_HEADS = 12
IMAGE_HEADS = 8
HEADS = 8


EPS = 1e-05
NEG = -1e30


BLOCK = 256
ALL = ("stream", "ring", "core")
OUTER = ("stream", "ring")


def partner(block, axis, stride):
    count = lax.axis_size(axis)
    route = []
    for low in range(count):
        high = low | 1 << stride
        if high != low and high < count:
            route += [(low, high), (high, low)]
    return lax.ppermute(block, axis, route)


def layer_norm(values, gain, bias):
    mean = jnp.mean(values, axis=-1, keepdims=True)
    centred = values - mean
    spread = jnp.mean(centred * centred, axis=-1, keepdims=True)
    return centred * lax.rsqrt(spread + EPS) * gain + bias


def exact_gelu(values):
    return jax.nn.gelu(values, approximate=False)


def matmul(left, right):
    return jnp.dot(left, right, preferred_element_type=jnp.float32)


def matmul_back(grad, weight):
    return jnp.einsum("psn,wn->psw", grad, weight, preferred_element_type=jnp.float32)


def weight_grad(inputs, grad):
    return jnp.einsum("psw,psn->wn", inputs, grad, preferred_element_type=jnp.float32)


def score_layout(rows, count):
    if count < rows:
        return ("phkq", 2)
    return ("phqk", 3)


def attend(query, keys, values, live, heads):
    pairs, rows, inner = query.shape
    count = keys.shape[1]
    size = inner // heads
    scale = size ** (-0.5)
    layout, key_axis = score_layout(rows, count)
    heads_q = query.reshape(pairs, rows, heads, size)
    heads_k = keys.reshape(pairs, count, heads, size)
    heads_v = values.reshape(pairs, count, heads, size)
    scores = (
        jnp.einsum("pqhd,pkhd->" + layout, heads_q, heads_k, preferred_element_type=jnp.float32)
        * scale
    )
    if key_axis == 2:
        shown = live[:, None, :, None]
    else:
        shown = live[:, None, None, :]
    scores = jnp.where(shown, scores, NEG)
    highest = jnp.max(scores, axis=key_axis, keepdims=True)
    expo = jnp.exp(scores - highest)
    probs = expo / jnp.sum(expo, axis=key_axis, keepdims=True)
    low_probs = probs.astype(jnp.bfloat16)
    mixed = jnp.einsum(
        layout + ",pkhd->pqhd", low_probs, heads_v, preferred_element_type=jnp.float32
    )
    kept = (probs, low_probs, heads_q, heads_k, heads_v, layout, key_axis)
    return (mixed.reshape(pairs, rows, inner).astype(jnp.bfloat16), kept)


def attend_back(d_mixed, kept):
    probs, low_probs, heads_q, heads_k, heads_v, layout, key_axis = kept
    pairs, rows, heads, size = heads_q.shape
    count = heads_k.shape[1]
    scale = size ** (-0.5)
    d_heads = d_mixed.reshape(pairs, rows, heads, size)
    d_probs = jnp.einsum(
        "pqhd,pkhd->" + layout, d_heads, heads_v, preferred_element_type=jnp.float32
    )
    d_values = jnp.einsum(
        layout + ",pqhd->pkhd", low_probs, d_heads, preferred_element_type=jnp.float32
    )
    weighted = jnp.sum(d_probs * probs, axis=key_axis, keepdims=True)
    d_scores = (probs * (d_probs - weighted)).astype(jnp.bfloat16)
    d_query = (
        jnp.einsum(layout + ",pkhd->pqhd", d_scores, heads_k, preferred_element_type=jnp.float32)
        * scale
    )
    d_keys = (
        jnp.einsum(layout + ",pqhd->pkhd", d_scores, heads_q, preferred_element_type=jnp.float32)
        * scale
    )
    d_kv = jnp.concatenate(
        [d_keys.reshape(pairs, count, heads * size), d_values.reshape(pairs, count, heads * size)],
        axis=-1,
    )
    return (
        d_query.reshape(pairs, rows, heads * size).astype(jnp.bfloat16),
        d_kv.astype(jnp.bfloat16),
    )


def self_forward(states, weights, live, heads):
    width = states.shape[-1]
    qkv = matmul(states, weights[9]).astype(jnp.bfloat16)
    mixed, attn_kept = attend(
        qkv[..., :width], qkv[..., width : 2 * width], qkv[..., 2 * width :], live, heads
    )
    branch = matmul(mixed, weights[10])
    base, norm_back = jax.vjp(
        layer_norm,
        states.astype(jnp.float32) + branch,
        weights[11].astype(jnp.float32),
        weights[12].astype(jnp.float32),
    )
    return (base, (mixed, attn_kept, norm_back))


def self_backward(d_base, kept, states, weights):
    mixed, attn_kept, norm_back = kept
    d_pre, d_gain, d_bias = norm_back(d_base)
    d_branch = d_pre.astype(jnp.bfloat16)
    grad_self_output = weight_grad(mixed, d_branch)
    d_mixed = matmul_back(d_branch, weights[10]).astype(jnp.bfloat16)
    d_query, d_kv = attend_back(d_mixed, attn_kept)
    d_qkv = jnp.concatenate([d_query, d_kv], axis=-1)
    grad_self_qkv = weight_grad(states, d_qkv)
    d_states = d_pre + matmul_back(d_qkv, weights[9])
    return (d_states, (grad_self_qkv, grad_self_output, d_gain, d_bias))


def stream_forward(base, low_base, weights, key_values, live):
    inner = weights[0].shape[1]
    query = matmul(low_base, weights[0]).astype(jnp.bfloat16)
    mixed, attn_kept = attend(query, key_values[..., :inner], key_values[..., inner:], live, HEADS)
    branch = matmul(mixed, weights[2])
    norm_values = tuple((piece.astype(jnp.float32) for piece in weights[5:9]))
    hidden, first_norm = jax.vjp(layer_norm, base + branch, norm_values[0], norm_values[1])
    low_hidden = hidden.astype(jnp.bfloat16)
    active, gelu_back = jax.vjp(exact_gelu, matmul(low_hidden, weights[3]))
    low_active = active.astype(jnp.bfloat16)
    result, second_norm = jax.vjp(
        layer_norm, hidden + matmul(low_active, weights[4]), norm_values[2], norm_values[3]
    )
    kept = (low_base, mixed, attn_kept, first_norm, low_hidden, gelu_back, low_active, second_norm)
    return (result, kept)


def stream_backward(d_result, kept, weights):
    low_base, mixed, attn_kept, first_norm, low_hidden, gelu_back, low_active, second_norm = kept
    d_raw, d_gain_two, d_bias_two = second_norm(d_result)
    d_down_in = d_raw.astype(jnp.bfloat16)
    grad_down = weight_grad(low_active, d_down_in)
    d_gate = gelu_back(matmul_back(d_down_in, weights[4]))[0].astype(jnp.bfloat16)
    grad_up = weight_grad(low_hidden, d_gate)
    d_hidden = d_raw + matmul_back(d_gate, weights[3])
    d_sum, d_gain_one, d_bias_one = first_norm(d_hidden)
    d_branch = d_sum.astype(jnp.bfloat16)
    grad_output = weight_grad(mixed, d_branch)
    d_mixed = matmul_back(d_branch, weights[2]).astype(jnp.bfloat16)
    d_query, d_kv = attend_back(d_mixed, attn_kept)
    grad_query = weight_grad(low_base, d_query)
    d_base = d_sum + matmul_back(d_query, weights[0])
    grads = (
        grad_query,
        grad_output,
        grad_up,
        grad_down,
        d_gain_one,
        d_bias_one,
        d_gain_two,
        d_bias_two,
    )
    return (d_base, d_kv, grads)


def to_blocks(piece):
    rows, columns = piece.shape
    cut = piece.reshape(rows, columns // BLOCK, BLOCK)
    return cut.transpose(1, 0, 2).reshape(-1, BLOCK)


def vector_rows(vectors):
    rows = []
    for group in (vectors[:6], vectors[6:]):
        line = jnp.concatenate(group, axis=-1)
        width = line.shape[-1]
        lead = [(0, 0)] * (line.ndim - 1)
        rows.append(jnp.pad(line, lead + [(0, BLOCK - width)]))
    stacked = jnp.stack(rows, axis=-2)
    lead = [(0, 0)] * (stacked.ndim - 2)
    return jnp.pad(stacked, lead + [(0, 6), (0, 0)])


def gather_pack(pieces, vectors=None):
    parts = [to_blocks(piece) for piece in pieces]
    if vectors is not None:
        parts.append(vector_rows(vectors))
    packed = jnp.concatenate(parts, axis=0)
    whole = lax.all_gather(packed, ALL, axis=0, tiled=True)
    shards = whole.shape[0] // packed.shape[0]
    whole = whole.reshape(shards, packed.shape[0], BLOCK)
    full = []
    at = 0
    for piece in pieces:
        rows, columns = piece.shape
        count = columns // BLOCK
        part = whole[:, at : at + rows * count].reshape(shards, count, rows, BLOCK)
        full.append(part.transpose(0, 2, 1, 3).reshape(shards * rows, columns))
        at += rows * count
    if vectors is not None:
        for line, group in ((0, vectors[:6]), (1, vectors[6:])):
            size = group[0].shape[0]
            part = whole[:, at + line, : 6 * size].reshape(shards, 6, size)
            full += list(part.transpose(1, 0, 2).reshape(6, shards * size))
    return full


def scatter_pack(grads, vectors=None):
    shards = lax.axis_size(ALL)
    cores = lax.axis_size("core")
    outer = shards // cores
    core = lax.axis_index("core")

    def side(at):
        parts = []
        for grad in grads:
            rows = grad.shape[0] // shards
            count = grad.shape[1] // BLOCK
            cut = grad.astype(jnp.bfloat16).reshape(outer, cores, rows, count, BLOCK)
            half = lax.dynamic_index_in_dim(cut, at, axis=1, keepdims=False)
            parts.append(half.transpose(0, 2, 1, 3).reshape(outer, count * rows, BLOCK))
        if vectors is not None:
            lines = [vector.reshape(shards, -1) for vector in vectors]
            rows = vector_rows(lines).reshape(outer, cores, 8, BLOCK)
            half = lax.dynamic_index_in_dim(rows, at, axis=1, keepdims=False)
            parts.append(half.astype(jnp.bfloat16))
        return jnp.concatenate(parts, axis=1)

    given = lax.ppermute(side(cores - 1 - core), "core", [(c, cores - 1 - c) for c in range(cores)])
    total = side(core).astype(jnp.float32) + given.astype(jnp.float32)
    total = total.astype(jnp.bfloat16)
    own = lax.psum_scatter(total, OUTER, scatter_dimension=0, tiled=True)[0].astype(jnp.float32)
    result = []
    at = 0
    for grad in grads:
        rows = grad.shape[0] // shards
        count = grad.shape[1] // BLOCK
        part = own[at : at + rows * count].reshape(count, rows, BLOCK)
        result.append(part.transpose(1, 0, 2).reshape(rows, count * BLOCK))
        at += rows * count
    if vectors is not None:
        for line, group in ((0, vectors[:6]), (1, vectors[6:])):
            size = group[0].shape[0] // shards
            result += list(own[at + line, : 6 * size].reshape(6, size))
    return result


def local(
    text_states,
    image_states,
    caption_lengths,
    region_counts,
    text_cotangent,
    image_cotangent,
    text_query,
    text_keyvalue,
    text_output,
    text_up,
    text_down,
    text_norm1_gain,
    text_norm1_bias,
    text_norm2_gain,
    text_norm2_bias,
    text_self_qkv,
    text_self_output,
    text_norm0_gain,
    text_norm0_bias,
    image_query,
    image_keyvalue,
    image_output,
    image_up,
    image_down,
    image_norm1_gain,
    image_norm1_bias,
    image_norm2_gain,
    image_norm2_bias,
    image_self_qkv,
    image_self_output,
    image_norm0_gain,
    image_norm0_bias,
):
    home = partner((image_states, image_cotangent, region_counts), "stream", 0)
    image_states, image_cotangent, region_counts = home
    first = gather_pack(
        (
            text_self_qkv,
            image_self_qkv,
            text_self_output,
            image_self_output,
            text_keyvalue,
            image_keyvalue,
            text_query,
            image_query,
        ),
        (
            text_norm1_gain,
            text_norm1_bias,
            text_norm2_gain,
            text_norm2_bias,
            text_norm0_gain,
            text_norm0_bias,
            image_norm1_gain,
            image_norm1_bias,
            image_norm2_gain,
            image_norm2_bias,
            image_norm0_gain,
            image_norm0_bias,
        ),
    )
    second = gather_pack(
        (text_output, image_output, text_up, image_up, text_down, image_down)
    )
    text_norms = first[8:14]
    image_norms = first[14:20]
    text_weights = (
        (first[6], first[4], second[0], second[2], second[4])
        + tuple(text_norms[:4])
        + (first[0], first[2])
        + tuple(text_norms[4:])
    )
    image_weights = (
        (first[7], first[5], second[1], second[3], second[5])
        + tuple(image_norms[:4])
        + (first[1], first[3])
        + tuple(image_norms[4:])
    )
    pairs = text_states.shape[0]
    slots = text_states.shape[1]
    regions = image_states.shape[1]
    text_live = lax.broadcasted_iota(jnp.int32, (pairs, slots), 1) < caption_lengths[:, None]
    region_live = lax.broadcasted_iota(jnp.int32, (pairs, regions), 1) < region_counts[:, None]
    text_base, text_self_kept = self_forward(text_states, text_weights, text_live, TEXT_HEADS)
    image_base, image_self_kept = self_forward(
        image_states, image_weights, region_live, IMAGE_HEADS
    )
    low_text = text_base.astype(jnp.bfloat16)
    low_image = image_base.astype(jnp.bfloat16)
    text_kv = matmul(low_text, text_weights[1]).astype(jnp.bfloat16)
    image_kv = matmul(low_image, image_weights[1]).astype(jnp.bfloat16)
    text_result, text_kept = stream_forward(
        text_base, low_text, text_weights, image_kv, region_live
    )
    image_result, image_kept = stream_forward(
        image_base, low_image, image_weights, text_kv, text_live
    )
    image_result = partner(image_result.astype(jnp.bfloat16), "stream", 0)
    d_text_base, d_image_kv, text_grads = stream_backward(
        text_cotangent.astype(jnp.float32), text_kept, text_weights
    )
    d_image_base, d_text_kv, image_grads = stream_backward(
        image_cotangent.astype(jnp.float32), image_kept, image_weights
    )
    early = scatter_pack(
        (
            text_grads[1],
            image_grads[1],
            text_grads[2],
            image_grads[2],
            text_grads[3],
            image_grads[3],
        )
    )
    text_kv_grad = weight_grad(low_text, d_text_kv)
    image_kv_grad = weight_grad(low_image, d_image_kv)
    d_text_base = d_text_base + matmul_back(d_text_kv, text_weights[1])
    d_image_base = d_image_base + matmul_back(d_image_kv, image_weights[1])
    d_text, text_self_grads = self_backward(d_text_base, text_self_kept, text_states, text_weights)
    d_image, image_self_grads = self_backward(
        d_image_base, image_self_kept, image_states, image_weights
    )
    d_image = partner(d_image, "stream", 0)
    late = scatter_pack(
        (
            text_self_grads[0],
            image_self_grads[0],
            text_self_grads[1],
            image_self_grads[1],
            text_kv_grad,
            image_kv_grad,
            text_grads[0],
            image_grads[0],
        ),
        tuple(text_grads[4:8])
        + tuple(text_self_grads[2:4])
        + tuple(image_grads[4:8])
        + tuple(image_self_grads[2:4]),
    )
    return (
        text_result.astype(jnp.bfloat16),
        image_result,
        d_text,
        d_image,
        late[6],
        late[4],
        early[0],
        early[2],
        early[4],
        late[8],
        late[9],
        late[10],
        late[11],
        late[0],
        late[2],
        late[12],
        late[13],
        late[7],
        late[5],
        early[1],
        early[3],
        early[5],
        late[14],
        late[15],
        late[16],
        late[17],
        late[1],
        late[3],
        late[18],
        late[19],
    )


def split_mesh(mesh):
    streams = mesh.shape["stream"]
    batch = mesh.shape["batch"]
    cores = 2 if batch % 2 == 0 else 1
    return Mesh(mesh.devices.reshape(streams, batch // cores, cores), ALL)


def solution(mesh):
    rank_three = P(ALL, None, None)
    rank_two = P(ALL, None)
    rank_one = P(ALL)
    stream_specs = (rank_two,) * 5 + (rank_one,) * 4 + (rank_two,) * 2 + (rank_one,) * 2
    return jax.shard_map(
        local,
        mesh=split_mesh(mesh),
        in_specs=(rank_three,) * 2
        + (rank_one,) * 2
        + (rank_three,) * 2
        + stream_specs
        + stream_specs,
        out_specs=(rank_three,) * 4 + stream_specs + stream_specs,
        check_vma=False,
    )
```

```python
import jax
import jax.numpy as jnp
from jax import lax
from jax.sharding import PartitionSpec as P

TEXT_HEADS = 12
IMAGE_HEADS = 8
HEADS = 8


EPS = 1e-05
NEG = -1e30


WIDTH = 768
ALL = ("stream", "batch")


def partner(block, axis, stride):
    count = lax.axis_size(axis)
    route = []
    for low in range(count):
        high = low | 1 << stride
        if high != low and high < count:
            route += [(low, high), (high, low)]
    return lax.ppermute(block, axis, route)


def layer_norm(values, gain, bias):
    mean = jnp.mean(values, axis=-1, keepdims=True)
    centred = values - mean
    spread = jnp.mean(centred * centred, axis=-1, keepdims=True)
    return centred * lax.rsqrt(spread + EPS) * gain + bias


def exact_gelu(values):
    return jax.nn.gelu(values, approximate=False)


def matmul(left, right):
    return jnp.dot(left, right, preferred_element_type=jnp.float32)


def matmul_back(grad, weight):
    return jnp.einsum("psn,wn->psw", grad, weight, preferred_element_type=jnp.float32)


def weight_grad(inputs, grad):
    return jnp.einsum("psw,psn->wn", inputs, grad, preferred_element_type=jnp.float32)


def score_layout(rows, count):
    if count < rows:
        return ("phkq", 2)
    return ("phqk", 3)


def attend(query, keys, values, live, heads):
    pairs, rows, inner = query.shape
    count = keys.shape[1]
    size = inner // heads
    scale = size ** (-0.5)
    layout, key_axis = score_layout(rows, count)
    heads_q = query.reshape(pairs, rows, heads, size)
    heads_k = keys.reshape(pairs, count, heads, size)
    heads_v = values.reshape(pairs, count, heads, size)
    scores = (
        jnp.einsum("pqhd,pkhd->" + layout, heads_q, heads_k, preferred_element_type=jnp.float32)
        * scale
    )
    if key_axis == 2:
        shown = live[:, None, :, None]
    else:
        shown = live[:, None, None, :]
    scores = jnp.where(shown, scores, NEG)
    highest = jnp.max(scores, axis=key_axis, keepdims=True)
    expo = jnp.exp(scores - highest)
    probs = expo / jnp.sum(expo, axis=key_axis, keepdims=True)
    low_probs = probs.astype(jnp.bfloat16)
    mixed = jnp.einsum(
        layout + ",pkhd->pqhd", low_probs, heads_v, preferred_element_type=jnp.float32
    )
    kept = (probs, low_probs, heads_q, heads_k, heads_v, layout, key_axis)
    return (mixed.reshape(pairs, rows, inner).astype(jnp.bfloat16), kept)


def attend_back(d_mixed, kept):
    probs, low_probs, heads_q, heads_k, heads_v, layout, key_axis = kept
    pairs, rows, heads, size = heads_q.shape
    count = heads_k.shape[1]
    scale = size ** (-0.5)
    d_heads = d_mixed.reshape(pairs, rows, heads, size)
    d_probs = jnp.einsum(
        "pqhd,pkhd->" + layout, d_heads, heads_v, preferred_element_type=jnp.float32
    )
    d_values = jnp.einsum(
        layout + ",pqhd->pkhd", low_probs, d_heads, preferred_element_type=jnp.float32
    )
    weighted = jnp.sum(d_probs * probs, axis=key_axis, keepdims=True)
    d_scores = (probs * (d_probs - weighted)).astype(jnp.bfloat16)
    d_query = (
        jnp.einsum(layout + ",pkhd->pqhd", d_scores, heads_k, preferred_element_type=jnp.float32)
        * scale
    )
    d_keys = (
        jnp.einsum(layout + ",pqhd->pkhd", d_scores, heads_q, preferred_element_type=jnp.float32)
        * scale
    )
    d_kv = jnp.concatenate(
        [d_keys.reshape(pairs, count, heads * size), d_values.reshape(pairs, count, heads * size)],
        axis=-1,
    )
    return (
        d_query.reshape(pairs, rows, heads * size).astype(jnp.bfloat16),
        d_kv.astype(jnp.bfloat16),
    )


def self_forward(states, weights, live, heads):
    width = states.shape[-1]
    qkv = matmul(states, weights[9]).astype(jnp.bfloat16)
    mixed, attn_kept = attend(
        qkv[..., :width], qkv[..., width : 2 * width], qkv[..., 2 * width :], live, heads
    )
    branch = matmul(mixed, weights[10])
    base, norm_back = jax.vjp(
        layer_norm,
        states.astype(jnp.float32) + branch,
        weights[11].astype(jnp.float32),
        weights[12].astype(jnp.float32),
    )
    return (base, (mixed, attn_kept, norm_back))


def self_backward(d_base, kept, states, weights):
    mixed, attn_kept, norm_back = kept
    d_pre, d_gain, d_bias = norm_back(d_base)
    d_branch = d_pre.astype(jnp.bfloat16)
    grad_self_output = weight_grad(mixed, d_branch)
    d_mixed = matmul_back(d_branch, weights[10]).astype(jnp.bfloat16)
    d_query, d_kv = attend_back(d_mixed, attn_kept)
    d_qkv = jnp.concatenate([d_query, d_kv], axis=-1)
    grad_self_qkv = weight_grad(states, d_qkv)
    d_states = d_pre + matmul_back(d_qkv, weights[9])
    return (d_states, (grad_self_qkv, grad_self_output, d_gain, d_bias))


def stream_forward(base, low_base, weights, key_values, live):
    inner = weights[0].shape[1]
    query = matmul(low_base, weights[0]).astype(jnp.bfloat16)
    mixed, attn_kept = attend(query, key_values[..., :inner], key_values[..., inner:], live, HEADS)
    branch = matmul(mixed, weights[2])
    norm_values = tuple((piece.astype(jnp.float32) for piece in weights[5:9]))
    hidden, first_norm = jax.vjp(layer_norm, base + branch, norm_values[0], norm_values[1])
    low_hidden = hidden.astype(jnp.bfloat16)
    active, gelu_back = jax.vjp(exact_gelu, matmul(low_hidden, weights[3]))
    low_active = active.astype(jnp.bfloat16)
    result, second_norm = jax.vjp(
        layer_norm, hidden + matmul(low_active, weights[4]), norm_values[2], norm_values[3]
    )
    kept = (low_base, mixed, attn_kept, first_norm, low_hidden, gelu_back, low_active, second_norm)
    return (result, kept)


def stream_backward(d_result, kept, weights):
    low_base, mixed, attn_kept, first_norm, low_hidden, gelu_back, low_active, second_norm = kept
    d_raw, d_gain_two, d_bias_two = second_norm(d_result)
    d_down_in = d_raw.astype(jnp.bfloat16)
    grad_down = weight_grad(low_active, d_down_in)
    d_gate = gelu_back(matmul_back(d_down_in, weights[4]))[0].astype(jnp.bfloat16)
    grad_up = weight_grad(low_hidden, d_gate)
    d_hidden = d_raw + matmul_back(d_gate, weights[3])
    d_sum, d_gain_one, d_bias_one = first_norm(d_hidden)
    d_branch = d_sum.astype(jnp.bfloat16)
    grad_output = weight_grad(mixed, d_branch)
    d_mixed = matmul_back(d_branch, weights[2]).astype(jnp.bfloat16)
    d_query, d_kv = attend_back(d_mixed, attn_kept)
    grad_query = weight_grad(low_base, d_query)
    d_base = d_sum + matmul_back(d_query, weights[0])
    grads = (
        grad_query,
        grad_output,
        grad_up,
        grad_down,
        d_gain_one,
        d_bias_one,
        d_gain_two,
        d_bias_two,
    )
    return (d_base, d_kv, grads)


def lane_slabs(piece, width):
    count = piece.shape[1] // width
    return [piece[:, k * width : (k + 1) * width] for k in range(count)]


def vector_rows(vectors, width):
    line = jnp.concatenate(vectors, axis=-1)
    short = -line.shape[-1] % width
    line = jnp.pad(line, [(0, 0)] * (line.ndim - 1) + [(0, short)])
    rows = line.reshape(line.shape[:-1] + (-1, width))
    below = -rows.shape[-2] % 8
    return jnp.pad(rows, [(0, 0)] * (rows.ndim - 2) + [(0, below), (0, 0)])


def vector_cut(rows, sizes):
    line = rows.reshape(rows.shape[:-2] + (-1,))
    pieces = []
    at = 0
    for size in sizes:
        pieces.append(line[..., at : at + size])
        at += size
    return pieces


def gather_pack(groups, vectors=()):
    parts = []
    for group in groups:
        joined = jnp.concatenate(group, axis=1)
        short = -joined.shape[1] % WIDTH
        parts += lane_slabs(jnp.pad(joined, ((0, 0), (0, short))), WIDTH)
    if vectors:
        parts.append(vector_rows(vectors, WIDTH))
    packed = jnp.concatenate(parts, axis=0)
    whole = lax.all_gather(packed, ALL, axis=0, tiled=True)
    shards = whole.shape[0] // packed.shape[0]
    whole = whole.reshape(shards, packed.shape[0], WIDTH)
    full = []
    at = 0
    for group in groups:
        rows = group[0].shape[0]
        columns = sum(piece.shape[1] for piece in group)
        slabs = []
        for _ in range(-(-columns // WIDTH)):
            slabs.append(whole[:, at : at + rows].reshape(shards * rows, WIDTH))
            at += rows
        joined = jnp.concatenate(slabs, axis=1)
        start = 0
        for piece in group:
            full.append(joined[:, start : start + piece.shape[1]])
            start += piece.shape[1]
    if vectors:
        pieces = vector_cut(whole[:, at:], [vector.shape[0] for vector in vectors])
        full += [piece.reshape(-1) for piece in pieces]
    return full


def halve(block, place, axis, bit):
    mine = (lax.axis_index(axis) >> bit) & 1
    route = [(at, at ^ (1 << bit)) for at in range(lax.axis_size(axis))]
    keep = lax.dynamic_index_in_dim(block, mine, axis=place)
    give = lax.dynamic_index_in_dim(block, 1 - mine, axis=place)
    got = lax.ppermute(give, axis, route)
    return keep.astype(jnp.float32) + got.astype(jnp.float32)


def scatter_pack(groups, width, stream_first, vectors=()):
    shards = lax.axis_size(ALL)
    bits = lax.axis_size("batch").bit_length() - 1
    parts = []
    for group in groups:
        joined = group[0] if len(group) == 1 else jnp.concatenate(group, axis=1)
        rows = joined.shape[0] // shards
        for slab in lane_slabs(joined, width):
            parts.append(slab.astype(jnp.bfloat16).reshape(shards, rows, width))
    if vectors:
        lines = [vector.reshape(shards, -1) for vector in vectors]
        parts.append(vector_rows(lines, width).astype(jnp.bfloat16))
    block = jnp.concatenate(parts, axis=1)
    block = block.reshape((2,) * (bits + 1) + block.shape[1:])
    order = [("batch", bit) for bit in range(bits)]
    order.insert(1 if stream_first else 2, ("stream", 0))
    for axis, bit in order:
        place = 0 if axis == "stream" else bits - bit
        block = halve(block.astype(jnp.bfloat16), place, axis, bit)
    own = block.reshape(block.shape[-2:])
    result = []
    at = 0
    for group in groups:
        rows = group[0].shape[0] // shards
        slabs = []
        for _ in range(sum(grad.shape[1] for grad in group) // width):
            slabs.append(own[at : at + rows])
            at += rows
        joined = slabs[0] if len(slabs) == 1 else jnp.concatenate(slabs, axis=1)
        start = 0
        for grad in group:
            result.append(joined[:, start : start + grad.shape[1]])
            start += grad.shape[1]
    if vectors:
        result += vector_cut(own[at:], [vector.shape[0] // shards for vector in vectors])
    return result


def local(
    text_states,
    image_states,
    caption_lengths,
    region_counts,
    text_cotangent,
    image_cotangent,
    text_query,
    text_keyvalue,
    text_output,
    text_up,
    text_down,
    text_norm1_gain,
    text_norm1_bias,
    text_norm2_gain,
    text_norm2_bias,
    text_self_qkv,
    text_self_output,
    text_norm0_gain,
    text_norm0_bias,
    image_query,
    image_keyvalue,
    image_output,
    image_up,
    image_down,
    image_norm1_gain,
    image_norm1_bias,
    image_norm2_gain,
    image_norm2_bias,
    image_self_qkv,
    image_self_output,
    image_norm0_gain,
    image_norm0_bias,
):
    home = partner((image_states, image_cotangent, region_counts), "stream", 0)
    image_states, image_cotangent, region_counts = home
    qkv_t, so_t, qt, kvt, qkv_i, so_i, kvi, qi, *norms = gather_pack(
        (
            (text_self_qkv,),
            (text_self_output,),
            (text_query, text_keyvalue),
            (image_self_qkv,),
            (image_self_output,),
            (image_keyvalue, image_query),
        ),
        (
            text_norm1_gain,
            text_norm1_bias,
            text_norm2_gain,
            text_norm2_bias,
            text_norm0_gain,
            text_norm0_bias,
            image_norm1_gain,
            image_norm1_bias,
            image_norm2_gain,
            image_norm2_bias,
            image_norm0_gain,
            image_norm0_bias,
        ),
    )
    out_t, up_t, down_t, out_i, up_i, down_i = gather_pack(
        ((text_output,), (text_up,), (text_down,), (image_output, image_up, image_down))
    )
    text_weights = (qt, kvt, out_t, up_t, down_t, *norms[:4], qkv_t, so_t, *norms[4:6])
    image_weights = (qi, kvi, out_i, up_i, down_i, *norms[6:10], qkv_i, so_i, *norms[10:])
    width = image_states.shape[2]
    pairs = text_states.shape[0]
    slots = text_states.shape[1]
    regions = image_states.shape[1]
    text_live = lax.broadcasted_iota(jnp.int32, (pairs, slots), 1) < caption_lengths[:, None]
    region_live = lax.broadcasted_iota(jnp.int32, (pairs, regions), 1) < region_counts[:, None]
    text_base, text_self_kept = self_forward(text_states, text_weights, text_live, TEXT_HEADS)
    image_base, image_self_kept = self_forward(
        image_states, image_weights, region_live, IMAGE_HEADS
    )
    low_text = text_base.astype(jnp.bfloat16)
    low_image = image_base.astype(jnp.bfloat16)
    text_kv = matmul(low_text, text_weights[1]).astype(jnp.bfloat16)
    image_kv = matmul(low_image, image_weights[1]).astype(jnp.bfloat16)
    text_result, text_kept = stream_forward(
        text_base, low_text, text_weights, image_kv, region_live
    )
    image_result, image_kept = stream_forward(
        image_base, low_image, image_weights, text_kv, text_live
    )
    image_result = partner(image_result.astype(jnp.bfloat16), "stream", 0)
    d_text_base, d_image_kv, text_grads = stream_backward(
        text_cotangent.astype(jnp.float32), text_kept, text_weights
    )
    d_image_base, d_text_kv, image_grads = stream_backward(
        image_cotangent.astype(jnp.float32), image_kept, image_weights
    )
    up_text, down_text = scatter_pack(((text_grads[2],), (text_grads[3],)), WIDTH, False)
    up_image, down_image = scatter_pack(((image_grads[2],), (image_grads[3],)), width, True)
    text_kv_grad = weight_grad(low_text, d_text_kv)
    image_kv_grad = weight_grad(low_image, d_image_kv)
    output_text, query_text, kv_text = scatter_pack(
        ((text_grads[1],), (text_grads[0], text_kv_grad)), WIDTH, False
    )
    output_image, query_image, kv_image = scatter_pack(
        ((image_grads[1],), (image_grads[0],), (image_kv_grad,)), width, True
    )
    d_text_base = d_text_base + matmul_back(d_text_kv, text_weights[1])
    d_image_base = d_image_base + matmul_back(d_image_kv, image_weights[1])
    d_text, text_self_grads = self_backward(d_text_base, text_self_kept, text_states, text_weights)
    d_image, image_self_grads = self_backward(
        d_image_base, image_self_kept, image_states, image_weights
    )
    d_image = partner(d_image, "stream", 0)
    qkv_text, so_text, *text_vectors = scatter_pack(
        ((text_self_grads[0],), (text_self_grads[1],)),
        WIDTH,
        False,
        (*text_grads[4:8], *text_self_grads[2:4]),
    )
    qkv_image, so_image, *image_vectors = scatter_pack(
        ((image_self_grads[0],), (image_self_grads[1],)),
        width,
        True,
        (*image_grads[4:8], *image_self_grads[2:4]),
    )
    return (
        text_result.astype(jnp.bfloat16),
        image_result,
        d_text,
        d_image,
        query_text,
        kv_text,
        output_text,
        up_text,
        down_text,
        *text_vectors[:4],
        qkv_text,
        so_text,
        *text_vectors[4:],
        query_image,
        kv_image,
        output_image,
        up_image,
        down_image,
        *image_vectors[:4],
        qkv_image,
        so_image,
        *image_vectors[4:],
    )


def solution(mesh):
    rank_three = P(ALL, None, None)
    rank_two = P(ALL, None)
    rank_one = P(ALL)
    stream_specs = (rank_two,) * 5 + (rank_one,) * 4 + (rank_two,) * 2 + (rank_one,) * 2
    return jax.shard_map(
        local,
        mesh=mesh,
        in_specs=(rank_three,) * 2
        + (rank_one,) * 2
        + (rank_three,) * 2
        + stream_specs
        + stream_specs,
        out_specs=(rank_three,) * 4 + stream_specs + stream_specs,
        check_vma=False,
    )
```

```python
import jax
import jax.numpy as jnp
from jax import lax
from jax.sharding import PartitionSpec as P

TEXT_HEADS = 12
IMAGE_HEADS = 8
HEADS = 8


EPS = 1e-05
NEG = -1e30


WIDTH = 768
ALL = ("stream", "batch")


def partner(block, axis, stride):
    count = lax.axis_size(axis)
    route = []
    for low in range(count):
        high = low | 1 << stride
        if high != low and high < count:
            route += [(low, high), (high, low)]
    return lax.ppermute(block, axis, route)


def layer_norm(values, gain, bias):
    mean = jnp.mean(values, axis=-1, keepdims=True)
    centred = values - mean
    spread = jnp.mean(centred * centred, axis=-1, keepdims=True)
    return centred * lax.rsqrt(spread + EPS) * gain + bias


def exact_gelu(values):
    return jax.nn.gelu(values, approximate=False)


def matmul(left, right):
    return jnp.dot(left, right, preferred_element_type=jnp.float32)


def matmul_back(grad, weight):
    return jnp.einsum("psn,wn->psw", grad, weight, preferred_element_type=jnp.float32)


def weight_grad(inputs, grad):
    return jnp.einsum("psw,psn->wn", inputs, grad, preferred_element_type=jnp.float32)


def score_layout(rows, count):
    if count < rows:
        return ("phkq", 2)
    return ("phqk", 3)


def attend(query, keys, values, live, heads):
    pairs, rows, inner = query.shape
    count = keys.shape[1]
    size = inner // heads
    scale = size ** (-0.5)
    layout, key_axis = score_layout(rows, count)
    heads_q = query.reshape(pairs, rows, heads, size)
    heads_k = keys.reshape(pairs, count, heads, size)
    heads_v = values.reshape(pairs, count, heads, size)
    scores = (
        jnp.einsum("pqhd,pkhd->" + layout, heads_q, heads_k, preferred_element_type=jnp.float32)
        * scale
    )
    if key_axis == 2:
        shown = live[:, None, :, None]
    else:
        shown = live[:, None, None, :]
    scores = jnp.where(shown, scores, NEG)
    highest = jnp.max(scores, axis=key_axis, keepdims=True)
    expo = jnp.exp(scores - highest)
    probs = expo / jnp.sum(expo, axis=key_axis, keepdims=True)
    low_probs = probs.astype(jnp.bfloat16)
    mixed = jnp.einsum(
        layout + ",pkhd->pqhd", low_probs, heads_v, preferred_element_type=jnp.float32
    )
    kept = (probs, low_probs, heads_q, heads_k, heads_v, layout, key_axis)
    return (mixed.reshape(pairs, rows, inner).astype(jnp.bfloat16), kept)


def attend_back(d_mixed, kept):
    probs, low_probs, heads_q, heads_k, heads_v, layout, key_axis = kept
    pairs, rows, heads, size = heads_q.shape
    count = heads_k.shape[1]
    scale = size ** (-0.5)
    d_heads = d_mixed.reshape(pairs, rows, heads, size)
    d_probs = jnp.einsum(
        "pqhd,pkhd->" + layout, d_heads, heads_v, preferred_element_type=jnp.float32
    )
    d_values = jnp.einsum(
        layout + ",pqhd->pkhd", low_probs, d_heads, preferred_element_type=jnp.float32
    )
    weighted = jnp.sum(d_probs * probs, axis=key_axis, keepdims=True)
    d_scores = (probs * (d_probs - weighted)).astype(jnp.bfloat16)
    d_query = (
        jnp.einsum(layout + ",pkhd->pqhd", d_scores, heads_k, preferred_element_type=jnp.float32)
        * scale
    )
    d_keys = (
        jnp.einsum(layout + ",pqhd->pkhd", d_scores, heads_q, preferred_element_type=jnp.float32)
        * scale
    )
    d_kv = jnp.concatenate(
        [d_keys.reshape(pairs, count, heads * size), d_values.reshape(pairs, count, heads * size)],
        axis=-1,
    )
    return (
        d_query.reshape(pairs, rows, heads * size).astype(jnp.bfloat16),
        d_kv.astype(jnp.bfloat16),
    )


def self_forward(states, weights, live, heads):
    width = states.shape[-1]
    qkv = matmul(states, weights[9]).astype(jnp.bfloat16)
    mixed, attn_kept = attend(
        qkv[..., :width], qkv[..., width : 2 * width], qkv[..., 2 * width :], live, heads
    )
    branch = matmul(mixed, weights[10])
    base, norm_back = jax.vjp(
        layer_norm,
        states.astype(jnp.float32) + branch,
        weights[11].astype(jnp.float32),
        weights[12].astype(jnp.float32),
    )
    return (base, (mixed, attn_kept, norm_back))


def self_mix_backward(d_base, kept, weights):
    mixed, _, norm_back = kept
    d_pre, d_gain, d_bias = norm_back(d_base)
    d_branch = d_pre.astype(jnp.bfloat16)
    grad_self_output = weight_grad(mixed, d_branch)
    d_mixed = matmul_back(d_branch, weights[10]).astype(jnp.bfloat16)
    return (d_pre, d_mixed, grad_self_output, (d_gain, d_bias))


def cross_forward(low_base, weights, key_values, live):
    inner = weights[0].shape[1]
    query = matmul(low_base, weights[0]).astype(jnp.bfloat16)
    return attend(query, key_values[..., :inner], key_values[..., inner:], live, HEADS)


def stream_forward(base, mixed, weights):
    branch = matmul(mixed, weights[2])
    norm_values = tuple((piece.astype(jnp.float32) for piece in weights[5:9]))
    hidden, first_norm = jax.vjp(layer_norm, base + branch, norm_values[0], norm_values[1])
    low_hidden = hidden.astype(jnp.bfloat16)
    active, gelu_back = jax.vjp(exact_gelu, matmul(low_hidden, weights[3]))
    low_active = active.astype(jnp.bfloat16)
    result, second_norm = jax.vjp(
        layer_norm, hidden + matmul(low_active, weights[4]), norm_values[2], norm_values[3]
    )
    return (result, (first_norm, low_hidden, gelu_back, low_active, second_norm))


def feed_backward(d_result, kept, weights):
    _, low_hidden, gelu_back, low_active, second_norm = kept
    d_raw, d_gain_two, d_bias_two = second_norm(d_result)
    d_down_in = d_raw.astype(jnp.bfloat16)
    grad_down = weight_grad(low_active, d_down_in)
    d_gate = gelu_back(matmul_back(d_down_in, weights[4]))[0].astype(jnp.bfloat16)
    grad_up = weight_grad(low_hidden, d_gate)
    d_hidden = d_raw + matmul_back(d_gate, weights[3])
    return (d_hidden, grad_up, grad_down, (d_gain_two, d_bias_two))


def mix_backward(d_hidden, mixed, kept, weights):
    d_sum, d_gain_one, d_bias_one = kept[0](d_hidden)
    d_branch = d_sum.astype(jnp.bfloat16)
    grad_output = weight_grad(mixed, d_branch)
    d_mixed = matmul_back(d_branch, weights[2]).astype(jnp.bfloat16)
    return (d_sum, d_mixed, grad_output, (d_gain_one, d_bias_one))


def lane_slabs(piece, width):
    count = piece.shape[1] // width
    return [piece[:, k * width : (k + 1) * width] for k in range(count)]


def vector_rows(vectors, width):
    line = jnp.concatenate(vectors, axis=-1)
    short = -line.shape[-1] % width
    line = jnp.pad(line, [(0, 0)] * (line.ndim - 1) + [(0, short)])
    rows = line.reshape(line.shape[:-1] + (-1, width))
    below = -rows.shape[-2] % 8
    return jnp.pad(rows, [(0, 0)] * (rows.ndim - 2) + [(0, below), (0, 0)])


def vector_cut(rows, sizes):
    line = rows.reshape(rows.shape[:-2] + (-1,))
    pieces = []
    at = 0
    for size in sizes:
        pieces.append(line[..., at : at + size])
        at += size
    return pieces


def gather_pack(groups, vectors=()):
    return gather_cut(gather_whole(groups, vectors), groups, vectors)


def gather_whole(groups, vectors=()):
    parts = []
    for group in groups:
        joined = jnp.concatenate(group, axis=1)
        short = -joined.shape[1] % WIDTH
        parts += lane_slabs(jnp.pad(joined, ((0, 0), (0, short))), WIDTH)
    if vectors:
        parts.append(vector_rows(vectors, WIDTH))
    packed = jnp.concatenate(parts, axis=0)
    whole = lax.all_gather(packed, ALL, axis=0, tiled=True)
    shards = whole.shape[0] // packed.shape[0]
    return whole.reshape(shards, packed.shape[0], WIDTH)


def gather_cut(whole, groups, vectors=()):
    shards = whole.shape[0]
    full = []
    at = 0
    for group in groups:
        rows = group[0].shape[0]
        columns = sum(piece.shape[1] for piece in group)
        slabs = []
        for _ in range(-(-columns // WIDTH)):
            slabs.append(whole[:, at : at + rows].reshape(shards * rows, WIDTH))
            at += rows
        joined = jnp.concatenate(slabs, axis=1)
        start = 0
        for piece in group:
            full.append(joined[:, start : start + piece.shape[1]])
            start += piece.shape[1]
    if vectors:
        pieces = vector_cut(whole[:, at:], [vector.shape[0] for vector in vectors])
        full += [piece.reshape(-1) for piece in pieces]
    return full


def halve(block, place, axis, bit):
    mine = (lax.axis_index(axis) >> bit) & 1
    route = [(at, at ^ (1 << bit)) for at in range(lax.axis_size(axis))]
    keep = lax.dynamic_index_in_dim(block, mine, axis=place)
    give = lax.dynamic_index_in_dim(block, 1 - mine, axis=place)
    got = lax.ppermute(give, axis, route)
    return keep.astype(jnp.float32) + got.astype(jnp.float32)


def scatter_pack(groups, width, vectors=()):
    shards = lax.axis_size(ALL)
    bits = lax.axis_size("batch").bit_length() - 1
    parts = []
    for group in groups:
        joined = group[0] if len(group) == 1 else jnp.concatenate(group, axis=1)
        rows = joined.shape[0] // shards
        for slab in lane_slabs(joined, width):
            parts.append(slab.astype(jnp.bfloat16).reshape(shards, rows, width))
    if vectors:
        lines = [vector.reshape(shards, -1) for vector in vectors]
        parts.append(vector_rows(lines, width).astype(jnp.bfloat16))
    block = jnp.concatenate(parts, axis=1)
    return block.reshape((2,) * (bits + 1) + block.shape[1:])


def reduce_steps(block, stream_first, begin, end=None):
    bits = lax.axis_size("batch").bit_length() - 1
    order = [("batch", bit) for bit in range(bits)]
    order.insert(1 if stream_first else 2, ("stream", 0))
    for axis, bit in order[begin:end]:
        place = 0 if axis == "stream" else bits - bit
        block = halve(block.astype(jnp.bfloat16), place, axis, bit)
    return block if end is None else block.astype(jnp.bfloat16)


def scatter_cut(block, groups, width, vectors=()):
    shards = lax.axis_size(ALL)
    own = block.reshape(block.shape[-2:])
    result = []
    at = 0
    for group in groups:
        rows = group[0].shape[0] // shards
        slabs = []
        for _ in range(sum(grad.shape[1] for grad in group) // width):
            slabs.append(own[at : at + rows])
            at += rows
        joined = slabs[0] if len(slabs) == 1 else jnp.concatenate(slabs, axis=1)
        start = 0
        for grad in group:
            result.append(joined[:, start : start + grad.shape[1]])
            start += grad.shape[1]
    if vectors:
        result += vector_cut(own[at:], [vector.shape[0] // shards for vector in vectors])
    return result


def local(
    text_states,
    image_states,
    caption_lengths,
    region_counts,
    text_cotangent,
    image_cotangent,
    text_query,
    text_keyvalue,
    text_output,
    text_up,
    text_down,
    text_norm1_gain,
    text_norm1_bias,
    text_norm2_gain,
    text_norm2_bias,
    text_self_qkv,
    text_self_output,
    text_norm0_gain,
    text_norm0_bias,
    image_query,
    image_keyvalue,
    image_output,
    image_up,
    image_down,
    image_norm1_gain,
    image_norm1_bias,
    image_norm2_gain,
    image_norm2_bias,
    image_self_qkv,
    image_self_output,
    image_norm0_gain,
    image_norm0_bias,
):
    home = partner((image_states, image_cotangent, region_counts), "stream", 0)
    image_states, image_cotangent, region_counts = home
    qkv_t, so_t, qt, kvt, qkv_i, so_i, kvi, qi, *norms = gather_pack(
        (
            (text_self_qkv,),
            (text_self_output,),
            (text_query, text_keyvalue),
            (image_self_qkv,),
            (image_self_output,),
            (image_keyvalue, image_query),
        ),
        (
            text_norm1_gain,
            text_norm1_bias,
            text_norm2_gain,
            text_norm2_bias,
            text_norm0_gain,
            text_norm0_bias,
            image_norm1_gain,
            image_norm1_bias,
            image_norm2_gain,
            image_norm2_bias,
            image_norm0_gain,
            image_norm0_bias,
        ),
    )
    later = ((text_output,), (text_up,), (text_down,), (image_output, image_up, image_down))
    whole = gather_whole(later)
    text_weights = (qt, kvt, None, None, None, *norms[:4], qkv_t, so_t, *norms[4:6])
    image_weights = (qi, kvi, None, None, None, *norms[6:10], qkv_i, so_i, *norms[10:])
    width = image_states.shape[2]
    pairs = text_states.shape[0]
    slots = text_states.shape[1]
    regions = image_states.shape[1]
    text_live = lax.broadcasted_iota(jnp.int32, (pairs, slots), 1) < caption_lengths[:, None]
    region_live = lax.broadcasted_iota(jnp.int32, (pairs, regions), 1) < region_counts[:, None]
    text_base, text_self_kept = self_forward(text_states, text_weights, text_live, TEXT_HEADS)
    image_base, image_self_kept = self_forward(
        image_states, image_weights, region_live, IMAGE_HEADS
    )
    low_text = text_base.astype(jnp.bfloat16)
    low_image = image_base.astype(jnp.bfloat16)
    text_kv = matmul(low_text, text_weights[1]).astype(jnp.bfloat16)
    image_kv = matmul(low_image, image_weights[1]).astype(jnp.bfloat16)
    text_mixed, text_attn = cross_forward(low_text, text_weights, image_kv, region_live)
    image_mixed, image_attn = cross_forward(low_image, image_weights, text_kv, text_live)
    whole, text_mixed, image_mixed = lax.optimization_barrier((whole, text_mixed, image_mixed))
    out_t, up_t, down_t, out_i, up_i, down_i = gather_cut(whole, later)
    text_weights = (*text_weights[:2], out_t, up_t, down_t, *text_weights[5:])
    image_weights = (*image_weights[:2], out_i, up_i, down_i, *image_weights[5:])
    text_result, text_kept = stream_forward(text_base, text_mixed, text_weights)
    image_result, image_kept = stream_forward(image_base, image_mixed, image_weights)
    image_result = partner(image_result.astype(jnp.bfloat16), "stream", 0)

    d_text, text_up_grad, text_down_grad, text_two = feed_backward(
        text_cotangent.astype(jnp.float32), text_kept, text_weights
    )
    d_image, image_up_grad, image_down_grad, image_two = feed_backward(
        image_cotangent.astype(jnp.float32), image_kept, image_weights
    )
    text_a = ((text_up_grad,), (text_down_grad,))
    image_a = ((image_up_grad,), (image_down_grad,))
    sum_ta = scatter_pack(text_a, WIDTH)
    sum_ia = scatter_pack(image_a, width)
    d_text, d_image, sum_ta, sum_ia = lax.optimization_barrier((d_text, d_image, sum_ta, sum_ia))
    sum_ta = reduce_steps(sum_ta, False, 0, 1)
    sum_ia = reduce_steps(sum_ia, True, 0, 1)

    d_text_sum, d_text_mixed, text_output_grad, text_one = mix_backward(
        d_text, text_mixed, text_kept, text_weights
    )
    d_image_sum, d_image_mixed, image_output_grad, image_one = mix_backward(
        d_image, image_mixed, image_kept, image_weights
    )
    d_text_mixed, d_image_mixed, sum_ta, sum_ia = lax.optimization_barrier(
        (d_text_mixed, d_image_mixed, sum_ta, sum_ia)
    )
    sum_ta = reduce_steps(sum_ta, False, 1, 2)
    sum_ia = reduce_steps(sum_ia, True, 1, 2)

    d_text_query, d_image_kv = attend_back(d_text_mixed, text_attn)
    d_image_query, d_text_kv = attend_back(d_image_mixed, image_attn)
    text_query_grad = weight_grad(low_text, d_text_query)
    image_query_grad = weight_grad(low_image, d_image_query)
    text_kv_grad = weight_grad(low_text, d_text_kv)
    image_kv_grad = weight_grad(low_image, d_image_kv)
    d_text = (
        d_text_sum
        + matmul_back(d_text_query, text_weights[0])
        + matmul_back(d_text_kv, text_weights[1])
    )
    d_image = (
        d_image_sum
        + matmul_back(d_image_query, image_weights[0])
        + matmul_back(d_image_kv, image_weights[1])
    )
    text_b = ((text_output_grad,), (text_query_grad, text_kv_grad))
    image_b = ((image_output_grad,), (image_query_grad,), (image_kv_grad,))
    sum_tb = scatter_pack(text_b, WIDTH)
    sum_ib = scatter_pack(image_b, width)
    d_text, d_image, sum_tb, sum_ib, sum_ta, sum_ia = lax.optimization_barrier(
        (d_text, d_image, sum_tb, sum_ib, sum_ta, sum_ia)
    )
    sum_ta = reduce_steps(sum_ta, False, 2, 3)
    sum_ia = reduce_steps(sum_ia, True, 2, 3)
    sum_tb = reduce_steps(sum_tb, False, 0, 1)
    sum_ib = reduce_steps(sum_ib, True, 0, 1)

    d_text_pre, d_text_self, text_so_grad, text_zero = self_mix_backward(
        d_text, text_self_kept, text_weights
    )
    d_image_pre, d_image_self, image_so_grad, image_zero = self_mix_backward(
        d_image, image_self_kept, image_weights
    )
    d_text_self, d_image_self, sum_tb, sum_ib = lax.optimization_barrier(
        (d_text_self, d_image_self, sum_tb, sum_ib)
    )
    sum_tb = reduce_steps(sum_tb, False, 1, 2)
    sum_ib = reduce_steps(sum_ib, True, 1, 2)

    d_image_qkv = jnp.concatenate(attend_back(d_image_self, image_self_kept[1]), axis=-1)
    d_text_qkv = jnp.concatenate(attend_back(d_text_self, text_self_kept[1]), axis=-1)
    image_qkv_grad = weight_grad(image_states, d_image_qkv)
    text_qkv_grad = weight_grad(text_states, d_text_qkv)
    text_vectors = (*text_one, *text_two, *text_zero)
    image_vectors = (*image_one, *image_two, *image_zero)
    text_c = ((text_qkv_grad,), (text_so_grad,))
    image_c = ((image_qkv_grad,), (image_so_grad,))
    sum_tc = scatter_pack(text_c, WIDTH, text_vectors)
    sum_ic = scatter_pack(image_c, width, image_vectors)
    d_text_qkv, d_image_qkv, sum_tc, sum_ic, sum_ta, sum_ia = lax.optimization_barrier(
        (d_text_qkv, d_image_qkv, sum_tc, sum_ic, sum_ta, sum_ia)
    )
    sum_tc = reduce_steps(sum_tc, False, 0, 1)
    sum_ic = reduce_steps(sum_ic, True, 0, 1)
    d_image = partner(d_image_pre + matmul_back(d_image_qkv, image_weights[9]), "stream", 0)
    d_text = d_text_pre + matmul_back(d_text_qkv, text_weights[9])
    sum_tc = reduce_steps(sum_tc, False, 1)
    sum_ic = reduce_steps(sum_ic, True, 1)
    sum_tb = reduce_steps(sum_tb, False, 2)
    sum_ib = reduce_steps(sum_ib, True, 2)
    sum_ta = reduce_steps(sum_ta, False, 3)
    sum_ia = reduce_steps(sum_ia, True, 3)
    up_text, down_text = scatter_cut(sum_ta, text_a, WIDTH)
    up_image, down_image = scatter_cut(sum_ia, image_a, width)
    output_text, query_text, kv_text = scatter_cut(sum_tb, text_b, WIDTH)
    output_image, query_image, kv_image = scatter_cut(sum_ib, image_b, width)
    qkv_text, so_text, *text_vectors = scatter_cut(sum_tc, text_c, WIDTH, text_vectors)
    qkv_image, so_image, *image_vectors = scatter_cut(sum_ic, image_c, width, image_vectors)
    return (
        text_result.astype(jnp.bfloat16),
        image_result,
        d_text,
        d_image,
        query_text,
        kv_text,
        output_text,
        up_text,
        down_text,
        *text_vectors[:4],
        qkv_text,
        so_text,
        *text_vectors[4:],
        query_image,
        kv_image,
        output_image,
        up_image,
        down_image,
        *image_vectors[:4],
        qkv_image,
        so_image,
        *image_vectors[4:],
    )


def solution(mesh):
    rank_three = P(ALL, None, None)
    rank_two = P(ALL, None)
    rank_one = P(ALL)
    stream_specs = (rank_two,) * 5 + (rank_one,) * 4 + (rank_two,) * 2 + (rank_one,) * 2
    return jax.shard_map(
        local,
        mesh=mesh,
        in_specs=(rank_three,) * 2
        + (rank_one,) * 2
        + (rank_three,) * 2
        + stream_specs
        + stream_specs,
        out_specs=(rank_three,) * 4 + stream_specs + stream_specs,
        check_vma=False,
    )
```
